128 devices in a mesh: row: 8 (over y, x_lo), col: 16 (over z, x_hi, core).
Axes of the slice: x: 4 (x_hi: 2, x_lo: 2; x = x_hi * 2 + x_lo), y: 4, z: 4, core: 2. Of those that a mesh axis runs over, the one named last changes fastest.
Arguments:
- filtered_bands: bfloat16 [4096, 16384], P(None, ('row', 'col')), may hold values from -0.09375 to 0.09375
Outputs:
- gram_upper: float32 [16384, 16384], P('row', 'col')
The draws below stay inside these ranges and needn't reach their ends.
All inputs are finite; a program needn't handle non-finite values.
Results may differ from the reference program's by a relative error of at most 0.0003.
Values may be sent and summed in bfloat16 or wider, within the bound.
No kernel may reach another device: no remote copies, remote signals or barrier semaphores. Data moves between devices by JAX's collectives and lax.ppermute only.
A program may use at most 128 MiB of HBM per device.

```python
import jax
import jax.numpy as jnp
from jax import lax

NB = 16384
G = 4096


def block_scale(own_key, shape, cuts, smallest, top_value):
    loudness = 1.0
    for axis_at, blocks in cuts:
        draws = jax.random.uniform(jax.random.fold_in(jax.random.fold_in(own_key, 6), axis_at), (blocks,), jnp.float32, smallest / len(cuts), top_value / len(cuts))
        loudness = loudness * jnp.repeat(jnp.exp(draws), shape[axis_at] // blocks).reshape((-1,) + (1,) * (len(shape) - 1 - axis_at))
    return loudness


def normal_values(rng, shape, scale, reach, cuts=(), dtype=jnp.bfloat16):
    loudness = block_scale(rng, shape, cuts, -0.22, 0.18) if cuts else 1.0
    array = jax.random.normal(rng, shape, jnp.float32) * scale * loudness
    return jnp.minimum(jnp.maximum(array, -reach), reach).astype(dtype)


def setup_inputs(seed: int = 0) -> dict:
    seeds = jax.random.split(jax.random.key(seed), 2)
    filtered_bands = normal_values(seeds[0], (G, NB), G ** -0.5, 0.09375, ((1, 128),))
    return dict(filtered_bands=filtered_bands)


def reference(filtered_bands):
    widened = filtered_bands.astype(jnp.float32)
    correlation = lax.dot_general(widened, widened, (((0,), (0,)), ((), ())), precision=lax.Precision.HIGHEST, preferred_element_type=jnp.float32)
    return jnp.triu(correlation)
```

```python
import functools

import jax
import jax.numpy as jnp
import numpy as np
from jax import lax
from jax.experimental import pallas as pl
from jax.experimental.pallas import tpu as pltpu
from jax.sharding import PartitionSpec as P


ROWS, COLS = 8, 16
BOTH = ("row", "col")


def coords(device):
    row, col = divmod(device, COLS)
    y, x_lo = divmod(row, 2)
    z, rest = divmod(col, 4)
    x_hi, core = divmod(rest, 2)
    return 2 * x_hi + x_lo, y, z, core


def device_at(x, y, z, core):
    x, y, z = x % 4, y % 4, z % 4
    return (y * 2 + x % 2) * COLS + z * 4 + (x // 2) * 2 + core


def moves(step):
    return {d: device_at(*step(*coords(d))) for d in range(ROWS * COLS)}


def transpose_moves():
    out = {}
    for k in range(ROWS):
        z_to, x_hi_to = divmod(k, 2)
        for s in range(COLS):
            z, x_hi, core = s // 4, (s // 2) % 2, s % 2
            shift = (0, 2, 1, 3)[(z % 2) * 2 + core]
            out[k * COLS + s] = device_at(2 * x_hi_to + (x_hi ^ core), z_to + shift, z_to, z // 2)
    return out


HOPS = (
    ("row_b", lambda x, y, z, c: (x + 2, y, z, c), "row_a", "row_a"),
    ("row_a_up", lambda x, y, z, c: (x, y, z + 1, c), "row_a", "row_a"),
    ("row_a_down", lambda x, y, z, c: (x, y, z - 1, c), "row_a", "row_a"),
    ("row_b_up", lambda x, y, z, c: (x, y, z + 1, c), "row_b", "row_b"),
    ("row_b_down", lambda x, y, z, c: (x, y, z - 1, c), "row_b", "row_b"),
    ("row_a_far", lambda x, y, z, c: (x, y, z + 1 - 2 * c, c), "row_a_up", "row_a_down"),
    ("row_b_far", lambda x, y, z, c: (x, y, z + 1 - 2 * c, c), "row_b_up", "row_b_down"),
    ("col_a", None, "row_a", "row_a"),
    ("col_b", lambda x, y, z, c: (x ^ 1, y, z, c), "col_a", "col_a"),
    ("col_a_up", lambda x, y, z, c: (x, y + 1, z, c), "col_a", "col_a"),
    ("col_a_down", lambda x, y, z, c: (x, y - 1, z, c), "col_a", "col_a"),
    ("col_b_up", lambda x, y, z, c: (x, y + 1, z, c), "col_b", "col_b"),
    ("col_b_down", lambda x, y, z, c: (x, y - 1, z, c), "col_b", "col_b"),
    ("col_a_far", lambda x, y, z, c: (x, y + 1 - 2 * c, z, c), "col_a_up", "col_a_down"),
    ("col_b_far", lambda x, y, z, c: (x ^ 1, y, z, c), "col_a_far", "col_a_far"),
)
ROW_NAMES = ("row_a", "row_b", "row_a_up", "row_a_down", "row_b_up", "row_b_down", "row_a_far", "row_b_far")
COL_NAMES = ("col_a", "col_b", "col_a_up", "col_a_down", "col_b_up", "col_b_down", "col_a_far", "col_b_far")
OTHER_CORE = sorted(moves(lambda x, y, z, c: (x, y, z, 1 - c)).items())


def active(device):
    row, col = divmod(device, COLS)
    return col // 2 >= row


@functools.cache
def plan():
    devices = range(ROWS * COLS)
    full = {n: transpose_moves() if step is None else moves(step) for n, step, _, _ in HOPS}
    holds = {"row_a": {d: d for d in devices}}
    for name, _, core0, core1 in HOPS:
        holds[name] = {t: holds[core1 if s % 2 else core0][s] for s, t in full[name].items()}
    needed = {n: set() for n in holds}
    for d in devices:
        if active(d):
            for n in ROW_NAMES:
                needed[n] |= {d, d ^ 1}
            for n in COL_NAMES:
                needed[n].add(d)
    pairs = {}
    for name, _, core0, core1 in reversed(HOPS):
        pairs[name] = sorted((s, t) for s, t in full[name].items() if t in needed[name])
        for s, _ in pairs[name]:
            needed[core1 if s % 2 else core0].add(s)
    places = np.zeros((ROWS * COLS, 24), np.int32)
    for d in devices:
        row, col = divmod(d, COLS)
        for i, n in enumerate(ROW_NAMES):
            assert holds[n][d] // COLS == row and holds[n][d ^ 1] // COLS == row
            places[d, 2 * i] = holds[n][d] % COLS
            places[d, 2 * i + 1] = holds[n][d ^ 1] % COLS
        for i, n in enumerate(COL_NAMES):
            assert holds[n][d] // COLS == col // 2 and holds[n][d] % COLS // 8 == col % 2
            places[d, 16 + i] = holds[n][d] % 8
        assert len(set(places[d, :16])) == 16 and len(set(places[d, 16:])) == 8
    return pairs, places


def tile_kernel(n_left, n_right, meta, *refs):
    left, right = refs[:n_left], refs[n_left : n_left + n_right]
    out, left_buf, right_buf, stage, left_sem, right_sem, out_sem = refs[-7:]
    n_pairs = n_left // 2
    row0, col0, is_active = meta[n_left + n_right], meta[n_left + n_right + 1], meta[n_left + n_right + 2]

    def left_copy(i):
        return pltpu.make_async_copy(
            left[i], left_buf.at[i // 2, :, pl.ds(i % 2 * 128, 128)], left_sem.at[i]
        )

    def right_copy(j):
        return pltpu.make_async_copy(right[j], right_buf.at[:, pl.ds(j * 128, 128)], right_sem.at[j])

    def out_copy(slot, i, half, j):
        place = meta[2 * i + half]
        return pltpu.make_async_copy(
            stage.at[slot, pl.ds(half * 128, 128), pl.ds(j * 128, 128)],
            out.at[
                pl.ds(pl.multiple_of(place * 128, 128), 128),
                pl.ds(pl.multiple_of(meta[n_left + j] * 128, 128), 128),
            ],
            out_sem.at[slot, half, j],
        )

    def each_out(slot, i, act):
        for half in range(2):
            for j in range(n_right):
                act(out_copy(slot, i, half, j))

    @pl.when(is_active == 1)
    def _():
        for j in range(n_right):
            right_copy(j).start()
        for i in range(n_left):
            left_copy(i).start()
        for j in range(n_right):
            right_copy(j).wait()

    @pl.when(is_active == 0)
    def _():
        stage[...] = jnp.zeros_like(stage)

    @pl.loop(0, n_pairs)
    def _(i):
        slot = i % 2

        @pl.when(i >= 2)
        def _():
            each_out(slot, i - 2, lambda c: c.wait())

        @pl.when(is_active == 1)
        def _():
            for half in range(2):
                pltpu.make_async_copy(
                    left[0], left_buf.at[i, :, pl.ds(half * 128, 128)], left_sem.at[2 * i + half]
                ).wait()
            product = lax.dot_general(
                left_buf[i], right_buf[...], (((0,), (0,)), ((), ())), preferred_element_type=jnp.float32
            )
            ahead = lax.broadcasted_iota(jnp.int32, (128, 128), 1) - lax.broadcasted_iota(jnp.int32, (128, 128), 0)
            for half in range(2):
                for j in range(n_right):
                    lag = row0 + meta[2 * i + half] * 128 - col0 - meta[n_left + j] * 128
                    block = product[half * 128 : half * 128 + 128, j * 128 : j * 128 + 128]
                    stage[slot, half * 128 : half * 128 + 128, j * 128 : j * 128 + 128] = jnp.where(
                        ahead >= lag, block, 0.0
                    )

        each_out(slot, i, lambda c: c.start())

    for i in range(max(n_pairs - 2, 0), n_pairs):
        each_out(i % 2, i, lambda c: c.wait())


def tile_part(meta, left, right, shape, previous=None):
    n_left, n_right = len(left), len(right)
    any_spec = pl.BlockSpec(memory_space=pl.ANY)
    extra = () if previous is None else (previous,)

    def kernel(meta, *refs):
        if extra:
            refs = refs[: n_left + n_right] + refs[n_left + n_right + 1 :]
        tile_kernel(n_left, n_right, meta, *refs)

    return pl.pallas_call(
        kernel,
        out_shape=jax.ShapeDtypeStruct(shape, jnp.float32),
        grid_spec=pltpu.PrefetchScalarGridSpec(
            num_scalar_prefetch=1,
            grid=(1,),
            in_specs=[any_spec] * (n_left + n_right + len(extra)),
            out_specs=any_spec,
            scratch_shapes=[
                pltpu.VMEM((n_left // 2, 4096, 256), jnp.bfloat16),
                pltpu.VMEM((4096, 128 * n_right), jnp.bfloat16),
                pltpu.VMEM((2, 256, 128 * n_right), jnp.float32),
                pltpu.SemaphoreType.DMA((n_left,)),
                pltpu.SemaphoreType.DMA((n_right,)),
                pltpu.SemaphoreType.DMA((2, 2, n_right)),
            ],
        ),
        input_output_aliases={1 + n_left + n_right: 0} if extra else {},
        compiler_params=pltpu.CompilerParams(vmem_limit_bytes=56 << 20),
        cost_estimate=pl.CostEstimate(
            flops=2 * 4096 * 128 * 128 * n_left * n_right,
            bytes_accessed=(n_left + n_right) * 4096 * 128 * 2 + n_left * n_right * 128 * 128 * 4,
            transcendentals=0,
        ),
    )(meta, *left, *right, *extra)


def shards(filtered_bands):
    pairs, places = plan()
    row, col = lax.axis_index("row"), lax.axis_index("col")
    core = col % 2
    shape = (filtered_bands.shape[1] * COLS, filtered_bands.shape[1] * ROWS)
    place = lax.dynamic_index_in_dim(jnp.asarray(places), row * COLS + col, 0, keepdims=False)
    held = {"row_a": filtered_bands}
    for name, _, core0, core1 in HOPS:
        sent = held[core0] if core0 == core1 else jnp.where(core == 0, held[core0], held[core1])
        held[name] = lax.ppermute(sent, BOTH, pairs[name])
    for name in ROW_NAMES:
        held["other_" + name] = lax.ppermute(held[name], BOTH, OTHER_CORE)

    ends = jnp.stack([row * shape[0], col * shape[1], (col // 2 >= row).astype(jnp.int32)])

    def part(row_names, col_names, previous=None):
        left = [h for n in row_names for h in (held[n], held["other_" + n])]
        right = [held[n] for n in col_names]
        picks = [2 * ROW_NAMES.index(n) + o for n in row_names for o in (0, 1)]
        picks += [16 + COL_NAMES.index(n) for n in col_names]
        meta = jnp.concatenate([place[np.array(picks)], ends])
        return tile_part(meta, left, right, shape, previous)

    return part(ROW_NAMES, COL_NAMES)


def solution(mesh):
    return jax.shard_map(
        shards,
        mesh=mesh,
        in_specs=(P(None, ("row", "col")),),
        out_specs=P("row", "col"),
        check_vma=False,
    )
```

```python
import functools

import jax
import jax.numpy as jnp
from jax import lax
from jax.experimental import pallas as pl
from jax.experimental.pallas import tpu as pltpu
from jax.sharding import PartitionSpec as P


ROWS, COLS = 8, 16
BOTH = ("row", "col")


def coords(device):
    row, col = divmod(device, COLS)
    y, x_lo = divmod(row, 2)
    z, rest = divmod(col, 4)
    x_hi, core = divmod(rest, 2)
    return 2 * x_hi + x_lo, y, z, core


def device_at(x, y, z, core):
    x, y, z = x % 4, y % 4, z % 4
    return (y * 2 + x % 2) * COLS + z * 4 + (x // 2) * 2 + core


def moves(step):
    return {d: device_at(*step(*coords(d))) for d in range(ROWS * COLS)}


def transpose_moves():
    out = {}
    for k in range(ROWS):
        z_to, x_hi_to = divmod(k, 2)
        for s in range(COLS):
            z, x_hi, core = s // 4, (s // 2) % 2, s % 2
            shift = (0, 2, 1, 3)[(z % 2) * 2 + core]
            out[k * COLS + s] = device_at(2 * x_hi_to + (x_hi ^ core), z_to + shift, z_to, z // 2)
    return out


HOPS = (
    ("row_b", lambda x, y, z, c: (x + 2, y, z, c), "row_a"),
    ("row_a_1", lambda x, y, z, c: (x, y, z + 1 - 2 * c, c), "row_a"),
    ("row_a_2", lambda x, y, z, c: (x, y, z - 1 + 2 * c, c), "row_a"),
    ("row_b_1", lambda x, y, z, c: (x, y, z + 1 - 2 * c, c), "row_b"),
    ("row_b_2", lambda x, y, z, c: (x, y, z - 1 + 2 * c, c), "row_b"),
    ("row_a_far", lambda x, y, z, c: (x, y, z + 1 - 2 * c, c), "row_a_1"),
    ("row_b_far", lambda x, y, z, c: (x, y, z + 1 - 2 * c, c), "row_b_1"),
    ("col_a", None, "row_a"),
    ("col_b", lambda x, y, z, c: (x ^ 1, y, z, c), "col_a"),
    ("col_a_1", lambda x, y, z, c: (x, y + 1 - 2 * c, z, c), "col_a"),
    ("col_a_2", lambda x, y, z, c: (x, y - 1 + 2 * c, z, c), "col_a"),
    ("col_b_1", lambda x, y, z, c: (x, y + 1 - 2 * c, z, c), "col_b"),
    ("col_b_2", lambda x, y, z, c: (x, y - 1 + 2 * c, z, c), "col_b"),
    ("col_a_far", lambda x, y, z, c: (x, y + 1 - 2 * c, z, c), "col_a_1"),
    ("col_b_far", lambda x, y, z, c: (x ^ 1, y, z, c), "col_a_far"),
)
ROW_NAMES = ("row_a", "row_b", "row_a_1", "row_a_2", "row_b_1", "row_b_2", "row_a_far", "row_b_far")
COL_NAMES = ("col_a", "col_b", "col_a_1", "col_a_2", "col_b_1", "col_b_2", "col_a_far", "col_b_far")
OTHER_CORE = sorted(moves(lambda x, y, z, c: (x, y, z, 1 - c)).items())


def hop_shift(name, core):
    return {"1": 2 * core - 1, "2": 1 - 2 * core, "far": 2}.get(name.split("_")[-1], 0)


def row_place(name, col, other):
    core = (col & 1) ^ other
    z = ((col >> 2) + hop_shift(name, core)) & 3
    return z * 4 + (((col >> 1) & 1) ^ (1 if "_b" in name else 0)) * 2 + core


def col_place(name, row, col):
    shift = ((row >> 1) + hop_shift(name, col & 1) - (col >> 2)) & 3
    core, z = shift >> 1, shift & 1
    return z * 4 + ((row & 1) ^ (1 if "_b" in name else 0) ^ core) * 2 + core


def active(row, col):
    return col // 2 >= row


@functools.cache
def plan():
    devices = range(ROWS * COLS)
    full = {n: transpose_moves() if step is None else moves(step) for n, step, _ in HOPS}
    holds = {"row_a": {d: d for d in devices}}
    for name, _, sent in HOPS:
        holds[name] = {t: holds[sent][s] for s, t in full[name].items()}
    needed = {n: set() for n in holds}
    for d in devices:
        row, col = divmod(d, COLS)
        for n in ROW_NAMES:
            for other in (0, 1):
                assert holds[n][d ^ other] == row * COLS + row_place(n, col, other)
        for n in COL_NAMES:
            assert holds[n][d] == col // 2 * COLS + col % 2 * 8 + col_place(n, row, col)
        if active(row, col):
            for n in ROW_NAMES:
                needed[n] |= {d, d ^ 1}
            for n in COL_NAMES:
                needed[n].add(d)
    pairs = {}
    for name, _, sent in reversed(HOPS):
        pairs[name] = sorted((s, t) for s, t in full[name].items() if t in needed[name])
        needed[sent] |= {s for s, _ in pairs[name]}
    return pairs


def tile_kernel(row_names, col_names, group, *refs):
    n_left, n_right = 2 * len(row_names), len(col_names)
    left, right = refs[:n_left], refs[n_left : n_left + n_right]
    out, left_buf, right_buf, stage, left_at, left_sem, right_sem, out_sem = refs[-8:]
    n_steps = n_left // group
    row, col = lax.axis_index("row"), lax.axis_index("col")
    is_active = active(row, col)
    row0, col0 = row * out.shape[0], col * out.shape[1]
    for i in range(n_left):
        left_at[i] = row_place(row_names[i // 2], col, i % 2)
    right_at = [col_place(n, row, col) for n in col_names]

    def left_copy(i):
        return pltpu.make_async_copy(
            left[i], left_buf.at[i // group, :, pl.ds(i % group * 128, 128)], left_sem.at[i]
        )

    def right_copy(j):
        return pltpu.make_async_copy(right[j], right_buf.at[:, pl.ds(j * 128, 128)], right_sem.at[j])

    def out_copy(slot, i, part, j):
        place = left_at[group * i + part]
        return pltpu.make_async_copy(
            stage.at[slot, pl.ds(part * 128, 128), pl.ds(j * 128, 128)],
            out.at[
                pl.ds(pl.multiple_of(place * 128, 128), 128),
                pl.ds(pl.multiple_of(right_at[j] * 128, 128), 128),
            ],
            out_sem.at[slot, part, j],
        )

    def each_out(slot, i, act):
        for part in range(group):
            for j in range(n_right):
                act(out_copy(slot, i, part, j))

    @pl.when(is_active)
    def _():
        for j in range(n_right):
            right_copy(j).start()
        for i in range(group):
            left_copy(i).start()
        for j in range(n_right):
            right_copy(j).wait()

    @pl.when(jnp.logical_not(is_active))
    def _():
        stage[...] = jnp.zeros_like(stage)

    @pl.loop(0, n_steps)
    def _(i):
        slot = i % 2

        @pl.when(i >= 2)
        def _():
            each_out(slot, i - 2, lambda c: c.wait())

        for step in range(1, n_steps):

            @pl.when(is_active & (i + 1 == step))
            def _():
                for part in range(group):
                    left_copy(step * group + part).start()

        @pl.when(is_active)
        def _():
            for part in range(group):
                pltpu.make_async_copy(
                    left[0], left_buf.at[i, :, pl.ds(part * 128, 128)], left_sem.at[group * i + part]
                ).wait()
            product = lax.dot_general(
                left_buf[i], right_buf[...], (((0,), (0,)), ((), ())), preferred_element_type=jnp.float32
            )
            ahead = lax.broadcasted_iota(jnp.int32, (128, 128), 1) - lax.broadcasted_iota(jnp.int32, (128, 128), 0)
            for part in range(group):
                for j in range(n_right):
                    lag = row0 + left_at[group * i + part] * 128 - col0 - right_at[j] * 128
                    block = product[part * 128 : part * 128 + 128, j * 128 : j * 128 + 128]
                    stage[slot, part * 128 : part * 128 + 128, j * 128 : j * 128 + 128] = jnp.where(
                        ahead >= lag, block, 0.0
                    )

        each_out(slot, i, lambda c: c.start())

    for i in range(max(n_steps - 2, 0), n_steps):
        each_out(i % 2, i, lambda c: c.wait())


def tile_part(row_names, col_names, held, shape, previous=None):
    left = [h for n in row_names for h in (held[n], held["other_" + n])]
    right = [held[n] for n in col_names]
    n_left, n_right = len(left), len(right)
    group = max(g for g in range(1, n_left + 1) if n_left % g == 0 and g * n_right <= 16)
    any_spec = pl.BlockSpec(memory_space=pl.ANY)
    extra = () if previous is None else (previous,)

    def kernel(*refs):
        if extra:
            refs = refs[: n_left + n_right] + refs[n_left + n_right + 1 :]
        tile_kernel(row_names, col_names, group, *refs)

    return pl.pallas_call(
        kernel,
        out_shape=jax.ShapeDtypeStruct(shape, jnp.float32),
        in_specs=[any_spec] * (n_left + n_right + len(extra)),
        out_specs=any_spec,
        scratch_shapes=[
            pltpu.VMEM((n_left // group, 4096, 128 * group), jnp.bfloat16),
            pltpu.VMEM((4096, 128 * n_right), jnp.bfloat16),
            pltpu.VMEM((2, 128 * group, 128 * n_right), jnp.float32),
            pltpu.SMEM((n_left,), jnp.int32),
            pltpu.SemaphoreType.DMA((n_left,)),
            pltpu.SemaphoreType.DMA((n_right,)),
            pltpu.SemaphoreType.DMA((2, group, n_right)),
        ],
        input_output_aliases={n_left + n_right: 0} if extra else {},
        compiler_params=pltpu.CompilerParams(vmem_limit_bytes=67043328),
        cost_estimate=pl.CostEstimate(
            flops=2 * 4096 * 128 * 128 * n_left * n_right,
            bytes_accessed=(n_left + n_right) * 4096 * 128 * 2 + n_left * n_right * 128 * 128 * 4,
            transcendentals=0,
        ),
    )(*left, *right, *extra)


def shards(filtered_bands):
    pairs = plan()
    shape = (filtered_bands.shape[1] * COLS, filtered_bands.shape[1] * ROWS)
    held = {"row_a": filtered_bands}
    for name, _, sent in HOPS:
        held[name] = lax.ppermute(held[sent], BOTH, pairs[name])
    for name in ROW_NAMES:
        held["other_" + name] = lax.ppermute(held[name], BOTH, OTHER_CORE)
    out = None
    for (row_names, col_names) in TILES.values():
        out = tile_part(row_names, col_names, held, shape, out)
    return out


TILES = {
    "tile_1": (("row_a", "row_b", "row_a_1", "row_a_2"), ("col_a", "col_b", "col_a_1", "col_a_2")),
    "tile_2": (("row_a_far", "row_b_1", "row_b_2", "row_b_far"), ("col_a", "col_b", "col_a_1", "col_a_2")),
    "tile_3": (ROW_NAMES, ("col_b_1", "col_b_2", "col_a_far", "col_b_far")),
}


def solution(mesh):
    return jax.shard_map(
        shards,
        mesh=mesh,
        in_specs=(P(None, ("row", "col")),),
        out_specs=P("row", "col"),
        check_vma=False,
    )
```

```python
import functools

import jax
import jax.numpy as jnp
from jax import lax
from jax.experimental import pallas as pl
from jax.experimental.pallas import tpu as pltpu
from jax.sharding import PartitionSpec as P


ROWS, COLS = 8, 16
BOTH = ("row", "col")


def coords(device):
    row, col = divmod(device, COLS)
    y, x_lo = divmod(row, 2)
    z, rest = divmod(col, 4)
    x_hi, core = divmod(rest, 2)
    return 2 * x_hi + x_lo, y, z, core


def device_at(x, y, z, core):
    x, y, z = x % 4, y % 4, z % 4
    return (y * 2 + x % 2) * COLS + z * 4 + (x // 2) * 2 + core


def moves(step):
    return {d: device_at(*step(*coords(d))) for d in range(ROWS * COLS)}


def transpose_moves():
    out = {}
    for k in range(ROWS):
        z_to, x_hi_to = divmod(k, 2)
        for s in range(COLS):
            z, x_hi, core = s // 4, (s // 2) % 2, s % 2
            shift = (0, 2, 1, 3)[(z % 2) * 2 + core]
            out[k * COLS + s] = device_at(2 * x_hi_to + (x_hi ^ core), z_to + shift, z_to, z // 2)
    return out


HOPS = (
    ("row_b", lambda x, y, z, c: (x + 2, y, z, c), "row_a"),
    ("row_a_1", lambda x, y, z, c: (x, y, z + 1 - 2 * c, c), "row_a"),
    ("row_a_2", lambda x, y, z, c: (x, y, z - 1 + 2 * c, c), "row_a"),
    ("row_b_1", lambda x, y, z, c: (x, y, z + 1 - 2 * c, c), "row_b"),
    ("row_b_2", lambda x, y, z, c: (x, y, z - 1 + 2 * c, c), "row_b"),
    ("row_a_far", lambda x, y, z, c: (x, y, z + 1 - 2 * c, c), "row_a_1"),
    ("row_b_far", lambda x, y, z, c: (x, y, z + 1 - 2 * c, c), "row_b_1"),
    ("col_a", None, "row_a"),
    ("col_b", lambda x, y, z, c: (x ^ 1, y, z, c), "col_a"),
    ("col_a_1", lambda x, y, z, c: (x, y + 1 - 2 * c, z, c), "col_a"),
    ("col_a_2", lambda x, y, z, c: (x, y - 1 + 2 * c, z, c), "col_a"),
    ("col_b_1", lambda x, y, z, c: (x, y + 1 - 2 * c, z, c), "col_b"),
    ("col_b_2", lambda x, y, z, c: (x, y - 1 + 2 * c, z, c), "col_b"),
    ("col_a_far", lambda x, y, z, c: (x, y + 1 - 2 * c, z, c), "col_a_1"),
    ("col_b_far", lambda x, y, z, c: (x ^ 1, y, z, c), "col_a_far"),
)
ROW_NAMES = ("row_a", "row_b", "row_a_1", "row_a_2", "row_b_1", "row_b_2", "row_a_far", "row_b_far")
COL_NAMES = ("col_a", "col_b", "col_a_1", "col_a_2", "col_b_1", "col_b_2", "col_a_far", "col_b_far")
OTHER_CORE = sorted(moves(lambda x, y, z, c: (x, y, z, 1 - c)).items())


def hop_shift(name, core):
    return {"1": 2 * core - 1, "2": 1 - 2 * core, "far": 2}.get(name.split("_")[-1], 0)


def row_place(name, col, other):
    core = (col & 1) ^ other
    z = ((col >> 2) + hop_shift(name, core)) & 3
    return z * 4 + (((col >> 1) & 1) ^ (1 if "_b" in name else 0)) * 2 + core


def col_place(name, row, col):
    shift = ((row >> 1) + hop_shift(name, col & 1) - (col >> 2)) & 3
    core, z = shift >> 1, shift & 1
    return z * 4 + ((row & 1) ^ (1 if "_b" in name else 0) ^ core) * 2 + core


def active(row, col):
    return col // 2 >= row


@functools.cache
def plan():
    devices = range(ROWS * COLS)
    full = {n: transpose_moves() if step is None else moves(step) for n, step, _ in HOPS}
    holds = {"row_a": {d: d for d in devices}}
    for name, _, sent in HOPS:
        holds[name] = {t: holds[sent][s] for s, t in full[name].items()}
    needed = {n: set() for n in holds}
    for d in devices:
        row, col = divmod(d, COLS)
        for n in ROW_NAMES:
            for other in (0, 1):
                assert holds[n][d ^ other] == row * COLS + row_place(n, col, other)
        for n in COL_NAMES:
            assert holds[n][d] == col // 2 * COLS + col % 2 * 8 + col_place(n, row, col)
        if active(row, col):
            for n in ROW_NAMES:
                needed[n] |= {d, d ^ 1}
            for n in COL_NAMES:
                needed[n].add(d)
    pairs = {}
    for name, _, sent in reversed(HOPS):
        pairs[name] = sorted((s, t) for s, t in full[name].items() if t in needed[name])
        needed[sent] |= {s for s, _ in pairs[name]}
    return pairs


def tile_kernel(row_names, col_names, group, early, *refs):
    n_left, sets = 2 * len(row_names), 2 if early else 1
    n_right, n_groups = len(col_names) // sets, n_left // group
    left, right = refs[:n_left], refs[n_left : n_left + sets * n_right]
    out, left_buf, right_buf, stage, left_at, right_at, left_sem, right_sem, out_sem = refs[-9:]
    row, col = lax.axis_index("row"), lax.axis_index("col")
    is_active = active(row, col)
    row0, col0 = row * out.shape[0], col * out.shape[1]
    for i in range(n_left):
        left_at[i] = row_place(row_names[i // 2], col, i % 2)
    for j, name in enumerate(col_names):
        right_at[j] = col_place(name, row, col)

    def left_copies(g):
        return [
            pltpu.make_async_copy(
                left[g * group + p], left_buf.at[g, :, pl.ds(p * 128, 128)], left_sem.at[g * group + p]
            )
            for p in range(group)
        ]

    def right_copies(r):
        return [
            pltpu.make_async_copy(
                right[r * n_right + j], right_buf.at[r, :, pl.ds(j * 128, 128)], right_sem.at[r * n_right + j]
            )
            for j in range(n_right)
        ]

    def start(copies):
        for c in copies:
            c.start()

    def wait(copies):
        for c in copies:
            c.wait()

    def job(step):
        return jnp.where(step < early, step, step - early), jnp.where(step < early, 0, sets - 1)

    def out_copies(slot, step):
        g, r = job(step)
        return [
            pltpu.make_async_copy(
                stage.at[slot, pl.ds(p * 128, 128), pl.ds(j * 128, 128)],
                out.at[
                    pl.ds(pl.multiple_of(left_at[g * group + p] * 128, 128), 128),
                    pl.ds(pl.multiple_of(right_at[r * n_right + j] * 128, 128), 128),
                ],
                out_sem.at[slot, p, j],
            )
            for p in range(group)
            for j in range(n_right)
        ]

    n_steps = early + n_groups
    first_left = [g if g < early else g + early for g in range(n_groups)]
    starts = {s: [] for s in range(-1, n_steps)}
    for g in range(n_groups):
        starts[g - 1].append(("left", g))
    starts[-1].append(("right", 0))
    if early:
        starts[0].append(("right", 1))
    reads = {s: [("left", g) for g in range(n_groups) if first_left[g] == s] for s in range(n_steps)}
    reads[0].append(("right", 0))
    if early:
        reads[early].append(("right", 1))

    def each(items, act):
        for kind, k in items:
            act(left_copies(k) if kind == "left" else right_copies(k))

    @pl.when(is_active)
    def _():
        each(starts[-1], start)

    @pl.when(jnp.logical_not(is_active))
    def _():
        stage[...] = jnp.zeros_like(stage)

    @pl.loop(0, n_steps)
    def _(step):
        slot = step % 2

        @pl.when(step >= 2)
        def _():
            wait(out_copies(slot, step - 2))

        for s in range(n_steps):

            @pl.when(is_active & (step == s))
            def _():
                each(starts[s], start)
                each(reads[s], wait)

        @pl.when(is_active)
        def _():
            g, r = job(step)
            product = lax.dot_general(
                left_buf[g], right_buf[r], (((0,), (0,)), ((), ())), preferred_element_type=jnp.float32
            )
            ahead = lax.broadcasted_iota(jnp.int32, (128, 128), 1) - lax.broadcasted_iota(jnp.int32, (128, 128), 0)
            for p in range(group):
                for j in range(n_right):
                    lag = row0 + left_at[g * group + p] * 128 - col0 - right_at[r * n_right + j] * 128
                    block = product[p * 128 : p * 128 + 128, j * 128 : j * 128 + 128]
                    stage[slot, p * 128 : p * 128 + 128, j * 128 : j * 128 + 128] = jnp.where(ahead >= lag, block, 0.0)

        start(out_copies(slot, step))

    for step in range(max(n_steps - 2, 0), n_steps):
        wait(out_copies(step % 2, step))


def tile_part(row_names, col_names, early_names, held, shape, previous=None):
    left = [h for n in row_names for h in (held[n], held["other_" + n])]
    right = [held[n] for n in col_names]
    n_left, n_all, sets = len(left), len(right), 2 if early_names else 1
    n_right, group = n_all // sets, 16 // (n_all // sets)
    depth = left[0].shape[0]
    units = n_left * n_right + 2 * early_names * n_right
    any_spec = pl.BlockSpec(memory_space=pl.ANY)
    extra = () if previous is None else (previous,)

    def kernel(*refs):
        if extra:
            refs = refs[: n_left + n_all] + refs[n_left + n_all + 1 :]
        tile_kernel(row_names, col_names, group, 2 * early_names // group, *refs)

    return pl.pallas_call(
        kernel,
        out_shape=jax.ShapeDtypeStruct(shape, jnp.float32),
        in_specs=[any_spec] * (n_left + n_all + len(extra)),
        out_specs=any_spec,
        scratch_shapes=[
            pltpu.VMEM((n_left // group, depth, 128 * group), jnp.bfloat16),
            pltpu.VMEM((sets, depth, 128 * n_right), jnp.bfloat16),
            pltpu.VMEM((2, 128 * group, 128 * n_right), jnp.float32),
            pltpu.SMEM((n_left,), jnp.int32),
            pltpu.SMEM((n_all,), jnp.int32),
            pltpu.SemaphoreType.DMA((n_left,)),
            pltpu.SemaphoreType.DMA((n_all,)),
            pltpu.SemaphoreType.DMA((2, group, n_right)),
        ],
        input_output_aliases={n_left + n_all: 0} if extra else {},
        compiler_params=pltpu.CompilerParams(vmem_limit_bytes=67043328),
        cost_estimate=pl.CostEstimate(
            flops=2 * depth * 128 * 128 * units,
            bytes_accessed=(n_left + n_all) * depth * 128 * 2 + units * 128 * 128 * 4,
            transcendentals=0,
        ),
    )(*left, *right, *extra)


def shards(filtered_bands):
    pairs = plan()
    shape = (filtered_bands.shape[1] * COLS, filtered_bands.shape[1] * ROWS)
    held = {"row_a": filtered_bands}
    for name, _, sent in HOPS:
        held[name] = lax.ppermute(held[sent], BOTH, pairs[name])
    for name in ROW_NAMES:
        held["other_" + name] = lax.ppermute(held[name], BOTH, OTHER_CORE)
    out = None
    for (row_names, col_names, early_names) in TILES.values():
        out = tile_part(row_names, col_names, early_names, held, shape, out)
    return out


TILES = {
    "tile_1": (
        ("row_a", "row_b", "row_a_1", "row_a_2", "row_b_1", "row_b_2"),
        ("col_a", "col_b", "col_a_1", "col_a_2"),
        0,
    ),
    "tile_2": (
        ("row_a_far", "row_b_far", "row_a", "row_b", "row_a_1", "row_a_2", "row_b_1", "row_b_2"),
        ("col_a", "col_b", "col_a_1", "col_a_2", "col_b_1", "col_b_2", "col_a_far", "col_b_far"),
        2,
    ),
}


def solution(mesh):
    return jax.shard_map(
        shards,
        mesh=mesh,
        in_specs=(P(None, ("row", "col")),),
        out_specs=P("row", "col"),
        check_vma=False,
    )
```
